32 devices in a mesh: layer: 8 (over y, x, core), tile: 4 (over z).
Axes of the slice: x: 2, y: 2, z: 4, core: 2. Of those that a mesh axis runs over, the one named last changes fastest.
Arguments:
- incident: bfloat16 [4096, 128], P('tile'), may hold values from -6 to 6
- interface: bfloat16 [16, 4096, 4096], P('layer', 'tile'), may hold values from -0.09375 to 0.09375
- eigvec: bfloat16 [16, 4096, 4096], P('layer', 'tile'), may hold values from -0.09375 to 0.09375
- angle: float32 [16, 4096], P('layer'), may hold values from -3.140625 to 3.140625
- decay: float32 [16, 4096], P('layer'), may hold values from 0.002 to 0.15
Outputs:
- fields: bfloat16 [16, 4096, 512], P('layer', 'tile')
- leaving: float32 [16, 4096, 128], P('layer', 'tile')
The draws below stay inside these ranges and needn't reach their ends.
All inputs are finite; a program needn't handle non-finite values.
Results may differ from the reference program's by a relative error of at most 0.035.
Values sent between devices are 32-bit elements; how exact they have to be, the bound alone decides.
A program may use at most 128 MiB of HBM per device.

```python
import math
import jax
import jax.numpy as jnp
from jax import lax

M = 4096
COLS = 64
DEPTHS = 4
LAYERS = 16


def steps_of(stream_key, extent, shards, least, top_value):
    def one(position, parts):
        heights = jax.random.uniform(jax.random.fold_in(jax.random.fold_in(stream_key, 6), position), (parts,), jnp.float32, least / len(shards), top_value / len(shards))
        return jnp.repeat(jnp.exp(heights), extent[position] // parts).reshape((-1,) + (1,) * (len(extent) - position - 1))

    factor_of = one(*shards[0])
    for cut in shards[1:]:
        factor_of = factor_of * one(*cut)
    return factor_of


def centred(own_key, dims, scale, limit, shards=(), held_as=jnp.bfloat16):
    gain = steps_of(own_key, dims, shards, -0.22, 0.18) if shards else 1.0
    entries = jax.random.normal(own_key, dims, jnp.float32) * scale * gain
    return jnp.minimum(jnp.maximum(entries, -limit), limit).astype(held_as)


def setup_inputs(seed: int = 0) -> dict:
    seeds = jax.random.split(jax.random.key(seed), 6)
    return {
        "incident": centred(seeds[0], (M, 2 * COLS), 1.0, 6.0, ((0, 4),)),
        "interface": centred(seeds[1], (LAYERS, M, M), ((M * 19) // 20) ** -0.5, 0.09375, ((0, 8), (1, 4))),
        "eigvec": centred(seeds[2], (LAYERS, M, M), M ** -0.5, 0.09375, ((0, 8), (1, 4))),
        "angle": jnp.clip(jax.random.uniform(seeds[3], (LAYERS, M), jnp.float32, -3.140625, 3.140625), -3.140625, 3.140625),
        "decay": jnp.clip(jnp.exp(math.log(0.15) - 4.317488 * jax.random.uniform(seeds[4], (LAYERS, M), jnp.float32) ** steps_of(seeds[4], (LAYERS, M), ((0, 8),), -0.2, 0.2)), 0.002, 0.15),
    }


def rotate(block, angle_row, decay_row, frac):
    values = block.astype(jnp.float32)
    half = values.shape[1] // 2
    real_part = values[:, :half]
    imag_part = values[:, half:]
    scale = jnp.exp(-frac * decay_row)
    cosine = (scale * jnp.cos(frac * angle_row))[:, None]
    sine = (scale * jnp.sin(frac * angle_row))[:, None]
    return jnp.concatenate([cosine * real_part - sine * imag_part, sine * real_part + cosine * imag_part], axis=1)


def reference(incident, interface, eigvec, angle, decay):
    def one_layer(enter, items):
        s_mat, w_mat, angle_row, decay_row = items
        phased = rotate(enter, angle_row, decay_row, 1.0).astype(jnp.bfloat16)
        leave = jnp.dot(s_mat, phased, preferred_element_type=jnp.float32)
        depth = jnp.concatenate([rotate(enter, angle_row, decay_row, step / DEPTHS).astype(jnp.bfloat16) for step in range(DEPTHS)], axis=1)
        field = jnp.dot(w_mat, depth, preferred_element_type=jnp.float32).astype(jnp.bfloat16)
        return leave, (field, leave)

    final, outputs = lax.scan(one_layer, incident.astype(jnp.float32), (interface, eigvec, angle, decay))
    return outputs[0], outputs[1]
```

```python
import functools

import jax
import jax.numpy as jnp
from jax import lax
from jax.experimental import pallas as pl
from jax.experimental.pallas import tpu as pltpu
from jax.sharding import PartitionSpec as P

DEPTHS = 4
WIDTH = 8
MESH = pl.DeviceIdType.MESH
NT = (((1,), (1,)), ((), ()))


def stack_kernel(
    groups, tiles, inc_ref, tab_ref, s_hbm, w_hbm, fields_ref, leave_ref,
    enter, sent, s_v, w_v, total, s_sem, w_sem, inc_send, send, recv,
):
    layers, blocks, width2, rows = sent.shape
    width = width2 // 2
    group = lax.axis_index("layer")
    tile = lax.axis_index("tile")
    toward = 1 - 2 * (tile // ((tiles + 1) // 2))

    def order(k):
        return lax.rem(tile + toward * k + tiles, tiles)

    def load(hbm, vmem, sem, j, t):
        cols = pl.ds(pl.multiple_of(t * rows, rows), rows)
        return pltpu.make_async_copy(hbm.at[j, :, cols], vmem.at[j, t], sem.at[j, t])

    for hbm, vmem, sem in ((s_hbm, s_v, s_sem), (w_hbm, w_v, w_sem)):
        for j in range(layers):
            for k in range(tiles):
                load(hbm, vmem, sem, j, order(k) if hbm is s_hbm else k).start()

    barrier = pltpu.get_barrier_semaphore()
    after = lax.rem(group + 1, groups)
    before = lax.rem(group + groups - 1, groups)
    for k in range(tiles):
        pl.semaphore_signal(barrier, inc=1, device_id=(after, order(k)), device_id_type=MESH)
        pl.semaphore_signal(barrier, inc=1, device_id=(before, order(k)), device_id_type=MESH)
        if k:
            pl.semaphore_signal(barrier, inc=1, device_id=(group, order(k)), device_id_type=MESH)
    pl.semaphore_wait(barrier, 3 * tiles - 1)

    def incident_copy(b, k):
        return pltpu.make_async_remote_copy(
            src_ref=inc_ref.at[b], dst_ref=enter.at[0, b, tile], send_sem=inc_send.at[b, k],
            recv_sem=recv.at[0, b, tile], device_id=(group, order(k)), device_id_type=MESH,
        )

    def leaving_copy(j, b, k):
        last = j == layers - 1
        return pltpu.make_async_remote_copy(
            src_ref=sent.at[j, b], dst_ref=enter.at[0 if last else j + 1, b, tile],
            send_sem=send.at[j, b, k], recv_sem=recv.at[0 if last else j + 1, b, tile],
            device_id=(after if last else group, order(k)), device_id_type=MESH,
        )

    def arrived(j, b, t):
        pltpu.make_async_copy(enter.at[j, b, t], enter.at[j, b, t], recv.at[j, b, t]).wait()

    def send_incident(b):
        for k in range(tiles - 1, 0, -1):
            incident_copy(b, k).start()
        pltpu.make_async_copy(inc_ref.at[b], enter.at[0, b, tile], recv.at[0, b, tile]).start()

    @pl.when(group == 0)
    def _():
        send_incident(0)

    def factors(j, t, step):
        row = 2 * (step - 1)
        return tab_ref[j, t, row : row + 1, :], tab_ref[j, t, row + 1 : row + 2, :]

    def through(j, b):
        def chunk(k, acc):
            t = order(k)

            @pl.when(b == 0)
            def _():
                load(s_hbm, s_v, s_sem, j, t).wait()

            if j == 0:
                arrived(j, b, t)
            else:
                @pl.when(k > 0)
                def _():
                    arrived(j, b, t)

            cosine, sine = factors(j, t, DEPTHS)
            real_part = enter[j, b, t, :width, :]
            imag_part = enter[j, b, t, width:, :]
            phased = jnp.concatenate(
                [cosine * real_part - sine * imag_part, sine * real_part + cosine * imag_part], axis=0
            ).astype(jnp.bfloat16)
            return acc + lax.dot_general(phased, s_v[j, t], NT, preferred_element_type=jnp.float32)

        acc = lax.fori_loop(0, tiles, chunk, jnp.zeros((width2, rows), jnp.float32))
        sent[j, b] = acc
        if j < layers - 1:
            enter[j + 1, b, tile] = acc
            for k in range(tiles - 1, 0, -1):
                leaving_copy(j, b, k).start()
        else:
            @pl.when(group < groups - 1)
            def _():
                for k in range(tiles - 1, -1, -1):
                    leaving_copy(j, b, k).start()

    def recover(j):
        def chunk(t, carry):
            load(w_hbm, w_v, w_sem, j, t).wait()
            real_part = jnp.concatenate([enter[j, b, t, :width, :] for b in range(blocks)], axis=0)
            imag_part = jnp.concatenate([enter[j, b, t, width:, :] for b in range(blocks)], axis=0)
            for step in range(DEPTHS):
                if step == 0:
                    parts = [real_part, imag_part]
                else:
                    cosine, sine = factors(j, t, step)
                    parts = [
                        cosine * real_part - sine * imag_part, sine * real_part + cosine * imag_part
                    ]
                depth = jnp.concatenate(parts, axis=0).astype(jnp.bfloat16)
                piece = lax.dot_general(depth, w_v[j, t], NT, preferred_element_type=jnp.float32)
                total[step] = jnp.where(t == 0, piece, total[step] + piece)
            return carry

        lax.fori_loop(0, tiles, chunk, 0)
        for step in range(DEPTHS):
            cols = 2 * width * blocks
            fields_ref[j, :, step * cols : (step + 1) * cols] = total[step].T.astype(jnp.bfloat16)

    def block_step(b, carry):
        for j in range(layers):
            through(j, b)
            if j == 0:
                @pl.when((group == 0) & (b < blocks - 1))
                def _():
                    send_incident(b + 1)
            if j < layers - 1:
                @pl.when(b == blocks - 1)
                def _():
                    recover(j)
        return carry

    total[...] = jnp.zeros_like(total)
    lax.fori_loop(0, blocks, block_step, 0)
    recover(layers - 1)
    for j in range(layers):
        real_part = jnp.concatenate([sent[j, b, :width, :] for b in range(blocks)], axis=0)
        imag_part = jnp.concatenate([sent[j, b, width:, :] for b in range(blocks)], axis=0)
        leave_ref[j] = jnp.concatenate([real_part, imag_part], axis=0).T

    def drain(b, carry):
        for j in range(layers - 1):
            for k in range(1, tiles):
                leaving_copy(j, b, k).wait_send()

        @pl.when(group < groups - 1)
        def _():
            for k in range(tiles):
                leaving_copy(layers - 1, b, k).wait_send()

        @pl.when(group == 0)
        def _():
            for k in range(1, tiles):
                incident_copy(b, k).wait_send()

        return carry

    lax.fori_loop(0, blocks, drain, 0)


def on_device(incident, interface, eigvec, angle, decay):
    groups = lax.axis_size("layer")
    tiles = lax.axis_size("tile")
    layers, rows, orders = interface.shape
    cols = incident.shape[1]
    blocks = cols // 2 // WIDTH
    amps = incident.astype(jnp.float32).T.reshape(2, blocks, WIDTH, rows)
    amps = amps.transpose(1, 0, 2, 3).reshape(blocks, 2 * WIDTH, rows)
    frac = (jnp.arange(1, DEPTHS + 1, dtype=jnp.float32) / DEPTHS)[None, :, None]
    scale = jnp.exp(-frac * decay[:, None, :])
    cosine = scale * jnp.cos(frac * angle[:, None, :])
    sine = scale * jnp.sin(frac * angle[:, None, :])
    table = jnp.stack([cosine, sine], axis=2).reshape(layers, 2 * DEPTHS, tiles, rows)
    table = table.transpose(0, 2, 1, 3)
    vmem = pl.BlockSpec(memory_space=pltpu.VMEM)
    anywhere = pl.BlockSpec(memory_space=pl.ANY)
    return pl.pallas_call(
        functools.partial(stack_kernel, groups, tiles),
        out_shape=(
            jax.ShapeDtypeStruct((layers, rows, DEPTHS * cols), jnp.bfloat16),
            jax.ShapeDtypeStruct((layers, rows, cols), jnp.float32),
        ),
        in_specs=[vmem, vmem, anywhere, anywhere],
        out_specs=(vmem, vmem),
        scratch_shapes=[
            pltpu.VMEM((layers, blocks, tiles, 2 * WIDTH, rows), jnp.float32),
            pltpu.VMEM((layers, blocks, 2 * WIDTH, rows), jnp.float32),
            pltpu.VMEM((layers, tiles, rows, rows), jnp.bfloat16),
            pltpu.VMEM((layers, tiles, rows, rows), jnp.bfloat16),
            pltpu.VMEM((DEPTHS, cols, rows), jnp.float32),
            pltpu.SemaphoreType.DMA((layers, tiles)),
            pltpu.SemaphoreType.DMA((layers, tiles)),
            pltpu.SemaphoreType.DMA((blocks, tiles)),
            pltpu.SemaphoreType.DMA((layers, blocks, tiles)),
            pltpu.SemaphoreType.DMA((layers, blocks, tiles)),
        ],
        compiler_params=pltpu.CompilerParams(
            collective_id=0, has_side_effects=True, vmem_limit_bytes=60 * 2**20
        ),
        name="stack",
    )(amps, table, interface, eigvec)


def solution(mesh):
    in_specs = (
        P("tile", None),
        P("layer", "tile", None),
        P("layer", "tile", None),
        P("layer", None),
        P("layer", None),
    )
    out_specs = (P("layer", "tile", None), P("layer", "tile", None))
    return jax.shard_map(
        on_device, mesh=mesh, in_specs=in_specs, out_specs=out_specs, check_vma=False
    )
```

```python
import functools

import jax
import jax.numpy as jnp
from jax import lax
from jax.experimental import pallas as pl
from jax.experimental.pallas import tpu as pltpu
from jax.sharding import PartitionSpec as P

DEPTHS = 4
WIDTH = 16
RELAY = True
MESH = pl.DeviceIdType.MESH
NT = (((1,), (1,)), ((), ()))


def stack_kernel(
    groups, tiles, inc_ref, tab_ref, s_hbm, w_hbm, fields_ref, leave_ref,
    enter, sent, s_v, w_v, total, s_sem, w_sem, inc_send, send, recv, pass_send,
):
    layers, blocks, width2, rows = sent.shape
    width = width2 // 2
    group = lax.axis_index("layer")
    tile = lax.axis_index("tile")
    toward = 1 - 2 * (tile // ((tiles + 1) // 2))

    end = (tile == 0) | (tile == tiles - 1)
    relays = RELAY and tiles > 3
    relay = (tile == 1) | (tile == tiles - 2)
    far = jnp.where(tile == 1, tiles - 1, 0)

    def order(k):
        return lax.rem(tile + toward * k + tiles, tiles)

    def load(hbm, vmem, sem, j, t):
        cols = pl.ds(pl.multiple_of(t * rows, rows), rows)
        return pltpu.make_async_copy(hbm.at[j, :, cols], vmem.at[j, t], sem.at[j, t])

    for hbm, vmem, sem in ((s_hbm, s_v, s_sem), (w_hbm, w_v, w_sem)):
        for j in range(layers):
            for k in range(tiles):
                load(hbm, vmem, sem, j, order(k) if hbm is s_hbm else k).start()

    barrier = pltpu.get_barrier_semaphore()
    after = lax.rem(group + 1, groups)
    before = lax.rem(group + groups - 1, groups)
    for k in range(tiles):
        pl.semaphore_signal(barrier, inc=1, device_id=(after, order(k)), device_id_type=MESH)
        pl.semaphore_signal(barrier, inc=1, device_id=(before, order(k)), device_id_type=MESH)
        if k:
            pl.semaphore_signal(barrier, inc=1, device_id=(group, order(k)), device_id_type=MESH)
    pl.semaphore_wait(barrier, 3 * tiles - 1)

    def incident_copy(b, k):
        return pltpu.make_async_remote_copy(
            src_ref=inc_ref.at[b], dst_ref=enter.at[0, b, tile], send_sem=inc_send.at[b, k],
            recv_sem=recv.at[0, b, tile], device_id=(group, order(k)), device_id_type=MESH,
        )

    def leaving_copy(j, b, k):
        last = j == layers - 1
        return pltpu.make_async_remote_copy(
            src_ref=sent.at[j, b], dst_ref=enter.at[0 if last else j + 1, b, tile],
            send_sem=send.at[j, b, k], recv_sem=recv.at[0 if last else j + 1, b, tile],
            device_id=(after if last else group, order(k)), device_id_type=MESH,
        )

    def arrived(j, b, t):
        pltpu.make_async_copy(enter.at[j, b, t], enter.at[j, b, t], recv.at[j, b, t]).wait()

    def passed_copy(j, b):
        return pltpu.make_async_remote_copy(
            src_ref=enter.at[j, b, far], dst_ref=enter.at[j, b, far], send_sem=pass_send.at[j, b],
            recv_sem=recv.at[j, b, far], device_id=(group, tiles - 1 - far), device_id_type=MESH,
        )

    def each_target(first, act):
        for k in range(tiles - 1, first - 1, -1):
            if relays and k == tiles - 1:
                @pl.when(jnp.logical_not(end))
                def _():
                    act(k)
            else:
                act(k)

    def send_incident(b):
        each_target(1, lambda k: incident_copy(b, k).start())
        pltpu.make_async_copy(inc_ref.at[b], enter.at[0, b, tile], recv.at[0, b, tile]).start()

    @pl.when(group == 0)
    def _():
        for b in range(1):
            send_incident(b)

    def factors(j, t, step):
        row = 2 * (step - 1)
        return tab_ref[j, t, row : row + 1, :], tab_ref[j, t, row + 1 : row + 2, :]

    def through(j, b):
        def chunk(k, acc):
            t = order(k)

            @pl.when(b == 0)
            def _():
                load(s_hbm, s_v, s_sem, j, t).wait()

            if j == 0:
                arrived(j, b, t)
            else:
                @pl.when(k > 0)
                def _():
                    arrived(j, b, t)

            if relays:
                @pl.when(relay & (t == far))
                def _():
                    passed_copy(j, b).start()

            cosine, sine = factors(j, t, DEPTHS)
            real_part = enter[j, b, t, :width, :]
            imag_part = enter[j, b, t, width:, :]
            phased = jnp.concatenate(
                [cosine * real_part - sine * imag_part, sine * real_part + cosine * imag_part], axis=0
            ).astype(jnp.bfloat16)
            return acc + lax.dot_general(phased, s_v[j, t], NT, preferred_element_type=jnp.float32)

        acc = lax.fori_loop(0, tiles, chunk, jnp.zeros((width2, rows), jnp.float32))
        sent[j, b] = acc
        if j < layers - 1:
            enter[j + 1, b, tile] = acc
            each_target(1, lambda k: leaving_copy(j, b, k).start())
        else:
            @pl.when(group < groups - 1)
            def _():
                each_target(0, lambda k: leaving_copy(j, b, k).start())

    def recover(j):
        def chunk(t, carry):
            load(w_hbm, w_v, w_sem, j, t).wait()
            real_part = jnp.concatenate([enter[j, b, t, :width, :] for b in range(blocks)], axis=0)
            imag_part = jnp.concatenate([enter[j, b, t, width:, :] for b in range(blocks)], axis=0)
            for step in range(DEPTHS):
                if step == 0:
                    parts = [real_part, imag_part]
                else:
                    cosine, sine = factors(j, t, step)
                    parts = [
                        cosine * real_part - sine * imag_part, sine * real_part + cosine * imag_part
                    ]
                depth = jnp.concatenate(parts, axis=0).astype(jnp.bfloat16)
                piece = lax.dot_general(depth, w_v[j, t], NT, preferred_element_type=jnp.float32)
                total[step] = jnp.where(t == 0, piece, total[step] + piece)
            return carry

        lax.fori_loop(0, tiles, chunk, 0)
        for step in range(DEPTHS):
            cols = 2 * width * blocks
            fields_ref[j, :, step * cols : (step + 1) * cols] = total[step].T.astype(jnp.bfloat16)

    def block_step(b, carry):
        for j in range(layers):
            through(j, b)
            if j == 0:
                @pl.when((group == 0) & (b < blocks - 1))
                def _():
                    send_incident(b + 1)
            if j < layers - 1:
                @pl.when(b == blocks - 1)
                def _():
                    recover(j)

        return carry

    total[...] = jnp.zeros_like(total)
    lax.fori_loop(0, blocks, block_step, 0)
    recover(layers - 1)
    for j in range(layers):
        real_part = jnp.concatenate([sent[j, b, :width, :] for b in range(blocks)], axis=0)
        imag_part = jnp.concatenate([sent[j, b, width:, :] for b in range(blocks)], axis=0)
        leave_ref[j] = jnp.concatenate([real_part, imag_part], axis=0).T

    def drain(b, carry):
        for j in range(layers - 1):
            each_target(1, lambda k: leaving_copy(j, b, k).wait_send())

        @pl.when(group < groups - 1)
        def _():
            each_target(0, lambda k: leaving_copy(layers - 1, b, k).wait_send())

        @pl.when(group == 0)
        def _():
            each_target(1, lambda k: incident_copy(b, k).wait_send())

        if relays:
            @pl.when(relay)
            def _():
                for j in range(layers):
                    passed_copy(j, b).wait_send()

        return carry

    lax.fori_loop(0, blocks, drain, 0)


def on_device(incident, interface, eigvec, angle, decay):
    groups = lax.axis_size("layer")
    tiles = lax.axis_size("tile")
    layers, rows, orders = interface.shape
    cols = incident.shape[1]
    blocks = cols // 2 // WIDTH
    amps = incident.astype(jnp.float32).T.reshape(2, blocks, WIDTH, rows)
    amps = amps.transpose(1, 0, 2, 3).reshape(blocks, 2 * WIDTH, rows)
    frac = (jnp.arange(1, DEPTHS + 1, dtype=jnp.float32) / DEPTHS)[None, :, None]
    scale = jnp.exp(-frac * decay[:, None, :])
    cosine = scale * jnp.cos(frac * angle[:, None, :])
    sine = scale * jnp.sin(frac * angle[:, None, :])
    table = jnp.stack([cosine, sine], axis=2).reshape(layers, 2 * DEPTHS, tiles, rows)
    table = table.transpose(0, 2, 1, 3)
    vmem = pl.BlockSpec(memory_space=pltpu.VMEM)
    anywhere = pl.BlockSpec(memory_space=pl.ANY)
    return pl.pallas_call(
        functools.partial(stack_kernel, groups, tiles),
        out_shape=(
            jax.ShapeDtypeStruct((layers, rows, DEPTHS * cols), jnp.bfloat16),
            jax.ShapeDtypeStruct((layers, rows, cols), jnp.float32),
        ),
        in_specs=[vmem, vmem, anywhere, anywhere],
        out_specs=(vmem, vmem),
        scratch_shapes=[
            pltpu.VMEM((layers, blocks, tiles, 2 * WIDTH, rows), jnp.float32),
            pltpu.VMEM((layers, blocks, 2 * WIDTH, rows), jnp.float32),
            pltpu.VMEM((layers, tiles, rows, rows), jnp.bfloat16),
            pltpu.VMEM((layers, tiles, rows, rows), jnp.bfloat16),
            pltpu.VMEM((DEPTHS, cols, rows), jnp.float32),
            pltpu.SemaphoreType.DMA((layers, tiles)),
            pltpu.SemaphoreType.DMA((layers, tiles)),
            pltpu.SemaphoreType.DMA((blocks, tiles)),
            pltpu.SemaphoreType.DMA((layers, blocks, tiles)),
            pltpu.SemaphoreType.DMA((layers, blocks, tiles)),
            pltpu.SemaphoreType.DMA((layers, blocks)),
        ],
        compiler_params=pltpu.CompilerParams(
            collective_id=0, has_side_effects=True, vmem_limit_bytes=60 * 2**20
        ),
        name="stack",
    )(amps, table, interface, eigvec)


def solution(mesh):
    in_specs = (
        P("tile", None),
        P("layer", "tile", None),
        P("layer", "tile", None),
        P("layer", None),
        P("layer", None),
    )
    out_specs = (P("layer", "tile", None), P("layer", "tile", None))
    return jax.shard_map(
        on_device, mesh=mesh, in_specs=in_specs, out_specs=out_specs, check_vma=False
    )
```
